128 devices in a mesh: rows: 32 (over x, z, core), cols: 4 (over y).
Axes of the slice: x: 4, y: 4, z: 4, core: 2. Of those that a mesh axis runs over, the one named last changes fastest.
Arguments:
- trailing: float32 [32768, 4096], P('rows', 'cols'), may hold values from -6 to 6
- leaf_v: float32 [32768, 512], P('rows', 'cols'), may hold values from -0.1875 to 0.1875
- leaf_t: float32 [16384, 512], P('rows', 'cols'), may hold values from -0.25 to 0.25
- merge_v: float32 [32768, 512], P('rows'), may hold values from -0.1875 to 0.1875
- merge_t: float32 [16384, 512], P('rows'), may hold values from -0.25 to 0.25
Outputs:
- updated: float32 [32768, 4096], P('rows', 'cols')
The draws below stay inside these ranges and needn't reach their ends.
All inputs are finite; a program needn't handle non-finite values.
Results may differ from the reference program's by a relative error of at most 0.00011.
Values sent between devices are 32-bit elements; how exact they have to be, the bound alone decides.
No kernel may reach another device: no remote copies, remote signals or barrier semaphores. Data moves between devices by JAX's collectives and lax.ppermute only.
A program may use at most 128 MiB of HBM per device.

```python
import jax
import jax.numpy as jnp
import numpy as np
from jax import lax

PANEL = 512
ROWS_DEV = 1024
NROWS_ALL = 32768
NCOLS_ALL = 4096
LEVELS = 5
N_ROWS = 32


def block_levels(rng, shape, pieces, low, largest):
    factor_of = 1.0
    for position, parts in pieces:
        draws = jax.random.uniform(jax.random.fold_in(jax.random.fold_in(rng, 6), position), (parts,), jnp.float32, low / len(pieces), largest / len(pieces))
        factor_of = factor_of * jnp.repeat(jnp.exp(draws), shape[position] // parts).reshape((-1,) + (1,) * (len(shape) - 1 - position))
    return factor_of


def scatter_about(rng, dims, deviation, limit, shards=(), dtype=jnp.bfloat16):
    gain = block_levels(rng, dims, shards, -0.22, 0.18) if shards else 1.0
    values = jax.random.normal(rng, dims, jnp.float32) * deviation * gain
    return jnp.minimum(jnp.maximum(values, -limit), limit).astype(dtype)


def setup_inputs(seed: int = 0) -> dict:
    streams_of = jax.random.split(jax.random.key(seed), 6)
    trailing = scatter_about(streams_of[0], (NROWS_ALL, NCOLS_ALL), 1.0, 6.0, ((0, 32), (1, 4)), jnp.float32)
    leaf_v = scatter_about(streams_of[1], (NROWS_ALL, PANEL), ROWS_DEV ** -0.5, 0.1875, ((0, 32), (1, 4)), jnp.float32)
    leaf_t = scatter_about(streams_of[2], (N_ROWS * PANEL, PANEL), PANEL ** -0.5, 0.25, ((0, 32), (1, 4)), jnp.float32)
    merge_v = scatter_about(streams_of[3], (N_ROWS * 2 * PANEL, PANEL), (2 * PANEL) ** -0.5, 0.1875, ((0, 32),), jnp.float32)
    merge_t = scatter_about(streams_of[4], (N_ROWS * PANEL, PANEL), PANEL ** -0.5, 0.25, ((0, 32),), jnp.float32)
    return {"trailing": trailing, "leaf_v": leaf_v, "leaf_t": leaf_t, "merge_v": merge_v, "merge_t": merge_t}


def reference(trailing, leaf_v, leaf_t, merge_v, merge_t):
    highest = lax.Precision.HIGHEST
    blocks = trailing.reshape(N_ROWS, ROWS_DEV, -1)
    vectors = leaf_v.reshape(N_ROWS, ROWS_DEV, PANEL)
    triangles = jnp.triu(leaf_t.reshape(N_ROWS, PANEL, PANEL))
    projected = jnp.einsum('nrk,nrc->nkc', vectors, blocks, precision=highest)
    weights = jnp.einsum('njk,njc->nkc', triangles, projected, precision=highest)
    blocks = blocks - jnp.einsum('nrk,nkc->nrc', vectors, weights, precision=highest)
    tops = blocks[:, :PANEL]
    remains = blocks[:, PANEL:]
    merge_vec = merge_v.reshape(N_ROWS, 2 * PANEL, PANEL)
    merge_tri = jnp.triu(merge_t.reshape(N_ROWS, PANEL, PANEL))
    for level in range(LEVELS):
        stride = 2 ** level
        uppers = np.arange(stride, N_ROWS, 2 * stride)
        lowers = uppers - stride
        upper_a = merge_vec[uppers, :PANEL]
        upper_b = merge_vec[uppers, PANEL:]
        factor = merge_tri[uppers]
        top_low = tops[lowers]
        top_up = tops[uppers]
        summed = jnp.einsum('njk,njc->nkc', upper_a, top_low, precision=highest) + jnp.einsum('njk,njc->nkc', upper_b, top_up, precision=highest)
        weight = jnp.einsum('njk,njc->nkc', factor, summed, precision=highest)
        new_low = top_low - jnp.einsum('njk,nkc->njc', upper_a, weight, precision=highest)
        new_up = top_up - jnp.einsum('njk,nkc->njc', upper_b, weight, precision=highest)
        tops = tops.at[lowers].set(new_low).at[uppers].set(new_up)
    return jnp.concatenate([tops, remains], axis=1).reshape(N_ROWS * ROWS_DEV, -1)
```

```python
import jax
import jax.numpy as jnp
from jax import lax
from jax.sharding import PartitionSpec as P


ROWS = range(32)


def bits(r):
    return r & 1, (r >> 1) & 3, r >> 3


def index(c, z, x):
    return (x % 4) * 8 + (z % 4) * 2 + c


def route(pick):
    pairs = []
    for r in ROWS:
        c, z, x = bits(r)
        to = pick(c, z, x)
        if to is not None:
            pairs.append((r, index(*to)))
    return pairs


SWAP_CORE = route(lambda c, z, x: (1 - c, z, x))
SWAP_Z1 = route(lambda c, z, x: (c, z ^ 1, x))
SWAP_Z2 = route(lambda c, z, x: (c, z ^ 2, x))
X_UP = route(lambda c, z, x: (c, z, x + 1) if x % 2 == 0 else None)
X_ONE_TWO = route(lambda c, z, x: (c, z, 2) if x == 1 else None)
X_THREE_TWO = route(lambda c, z, x: (c, z, 2) if x == 3 else None)
X_HOME = route(lambda c, z, x: (c, z, 0) if x == 2 else None)
Z_DOWN = route(lambda c, z, x: (c, z - 1, x) if c == 0 else None)
Z_UP_EVEN = route(lambda c, z, x: (c, z + 1, x) if c == 0 and z % 2 == 0 else None)
Z_UP_ODD = route(lambda c, z, x: (c, z + 1, x) if c == 0 and z % 2 == 1 else None)
CORE_UP = route(lambda c, z, x: (1, z, x) if c == 0 else None)


def move(block, pairs):
    return lax.ppermute(block, "rows", pairs)


def turn(block, by):
    count = lax.axis_size("cols")
    return lax.ppermute(block, "cols", [(i, (i + by) % count) for i in range(count)])


def mult(left, right):
    return jnp.dot(left, right, precision=lax.Precision.HIGH, preferred_element_type=jnp.float32)


def merge(mats, low, up):
    vec_a, vec_b, factor = mats[:512], mats[512:1024], jnp.triu(mats[1024:])
    summed = mult(vec_a.T, low) + mult(vec_b.T, up)
    weight = mult(factor.T, summed)
    return low - mult(vec_a, weight), up - mult(vec_b, weight)


def spread(top, bit, pairs):
    half = top.shape[1] // 2
    first, second = top[:, :half], top[:, half:]
    keep = jnp.where(bit == 0, first, second)
    got = move(jnp.where(bit == 0, second, first), pairs)
    return jnp.where(bit == 0, keep, got), jnp.where(bit == 0, got, keep)


def gather(low, up, bit, pairs):
    got = move(jnp.where(bit == 0, up, low), pairs)
    keep = jnp.where(bit == 0, low, up)
    return jnp.where(bit == 0, jnp.concatenate([keep, got], 1), jnp.concatenate([got, keep], 1))


def on_device(trailing, leaf_v, leaf_t, merge_v, merge_t):
    panel = leaf_t.shape[0]
    me = lax.axis_index("rows")
    col = lax.axis_index("cols")
    core, z, x = bits(me)
    leaf = jnp.concatenate([leaf_v, leaf_t], 0)
    half = leaf.shape[0] // 2
    mine = jnp.concatenate([merge_v, merge_t], 0)
    before = turn(leaf, 1)
    after = turn(leaf, -1)
    other_core = move(mine, SWAP_CORE)
    above = move(mine, Z_DOWN)
    from_even = move(mine, Z_UP_EVEN)
    far = jnp.concatenate([turn(before[:half], 1), turn(after[half:], -1)], 0)
    relayed = move(from_even, Z_UP_ODD)
    second = jnp.where(z % 2 == 1, from_even, relayed)
    above_1 = move(above, CORE_UP)
    second_1 = move(second, CORE_UP)
    own = jnp.where(core == 0, mine, other_core)
    above = jnp.where(core == 0, above, above_1)
    second = jnp.where(core == 0, second, second_1)
    mats0 = jnp.where(core == 1, mine, other_core)
    mats1 = jnp.where(z % 2 == 1, own, above)
    mats2 = jnp.where(z == 1, above, jnp.where(z == 2, own, second))
    mats3 = jnp.where(z == 0, own, jnp.where(z == 3, above, second))

    shards = [leaf, after, far, before]
    vectors = jnp.concatenate([s[:1024] for s in shards], 1)
    rows = lax.broadcasted_iota(jnp.int32, (panel, panel // 4), 0)
    cols = lax.broadcasted_iota(jnp.int32, (panel, panel // 4), 1)
    parts = [
        jnp.where(rows <= cols + ((col + i) % 4) * (panel // 4), s[1024:], 0.0)
        for i, s in enumerate(shards)
    ]
    triangle = jnp.concatenate(parts, 1)
    triangle = lax.dynamic_slice_in_dim(
        jnp.concatenate([triangle, triangle], 0), col * (panel // 4), panel, 0
    )
    projected = mult(vectors.T, trailing)
    weights = mult(triangle.T, projected)
    top = trailing[:panel] - mult(vectors[:panel], weights)
    remains = trailing[panel:] - mult(vectors[panel:], weights)

    low0, up0 = merge(mats0, *spread(top, core, SWAP_CORE))
    low1, up1 = merge(mats1, *spread(low0, z % 2, SWAP_Z1))
    low2, up2 = merge(mats2, *spread(low1, z // 2, SWAP_Z2))
    low3, up3 = merge(mats3, move(low2, X_UP), low2)
    low4, up4 = merge(mats3, move(low3, X_ONE_TWO), move(low3, X_THREE_TWO))
    home = move(low4, X_HOME)
    done = jnp.where(x == 0, home, jnp.where(x == 2, up4, up3))
    done = gather(done, up2, z // 2, SWAP_Z2)
    done = gather(done, up1, z % 2, SWAP_Z1)
    done = gather(done, up0, core, SWAP_CORE)
    return jnp.concatenate([done, remains], axis=0)


def solution(mesh):
    return jax.shard_map(
        on_device,
        mesh=mesh,
        in_specs=(
            P("rows", "cols"),
            P("rows", "cols"),
            P("rows", "cols"),
            P("rows", None),
            P("rows", None),
        ),
        out_specs=P("rows", "cols"),
        check_vma=False,
    )
```

```python
import functools

import jax
import jax.numpy as jnp
from jax import lax
from jax.experimental import pallas as pl
from jax.experimental.pallas import tpu as pltpu
from jax.sharding import PartitionSpec as P


F32 = jnp.float32
BF16 = jnp.bfloat16
PANEL = 512
SET_ROWS = 1408
ANY = pl.BlockSpec(memory_space=pl.ANY)
VMEM = pl.BlockSpec(memory_space=pltpu.VMEM)


def route(pick):
    pairs = []
    for r in range(32):
        c, z, x = r & 1, (r >> 1) & 3, r >> 3
        to = pick(c, z, x)
        if to is not None:
            c, z, x = to
            pairs.append((r, (x % 4) * 8 + (z % 4) * 2 + c))
    return pairs


SWAP_CORE = route(lambda c, z, x: (1 - c, z, x))
CORE_UP = route(lambda c, z, x: (1, z, x) if c == 0 else None)
CORE_DOWN = route(lambda c, z, x: (0, z, x) if c == 1 else None)
Z_UP_0 = route(lambda c, z, x: (c, z + 1, x) if c == 0 else None)
Z_DOWN_0 = route(lambda c, z, x: (c, z - 1, x) if c == 0 else None)
Z_TURN = {k: route(lambda c, z, x: (c, z + k, x)) for k in (1, 2, 3)}
Z_EARLY = {k: route(lambda c, z, x: (c, z + k, x) if (z + k) % 4 else None) for k in (1, 2, 3)}
Z_LATE = {k: route(lambda c, z, x: (c, z + k, x) if (z + k) % 4 == 0 else None) for k in (1, 2, 3)}
X_UP = route(lambda c, z, x: (c, z, x + 1) if x % 2 == 0 else None)
X_ONE_TWO = route(lambda c, z, x: (c, z, 2) if x == 1 else None)
X_THREE_TWO = route(lambda c, z, x: (c, z, 2) if x == 3 else None)
X_HOME = route(lambda c, z, x: (c, z, 0) if x == 2 else None)


def move(block, pairs):
    return lax.ppermute(block, "rows", pairs)


def turn(block, by):
    count = lax.axis_size("cols")
    return lax.ppermute(block, "cols", [(i, (i + by) % count) for i in range(count)])


def behind(block, *others):
    return lax.optimization_barrier((block, *others))[0]


def split(block):
    high = block.astype(BF16)
    return high, (block - high.astype(F32)).astype(BF16)


def dot(left, right):
    return jnp.dot(left, right, preferred_element_type=F32)


def dot3(left, right):
    (lh, ll), (rh, rl) = left, right
    return dot(lh, rh) + (dot(lh, rl) + dot(ll, rh))


def place():
    me = lax.axis_index("rows")
    return me % 2, (me // 2) % 4, me // 8


def shape(*dims, dtype=F32):
    return jax.ShapeDtypeStruct(dims, dtype)


def call(body, outs, flops, moved, mib, **options):
    return pl.pallas_call(
        body,
        out_shape=outs,
        cost_estimate=pl.CostEstimate(flops=flops, bytes_accessed=moved, transcendentals=0),
        compiler_params=pltpu.CompilerParams(vmem_limit_bytes=mib << 20),
        **options,
    )


def pack_leaf_body(v, t, out):
    out[:1024] = v[...]
    out[1024:] = t[...]


def pack_leaf(v, t):
    return call(pack_leaf_body, shape(1536, 128), 0, 3 << 19, 4)(v, t)


def pack_set_body(v, t, out):
    out[:1024] = v[...]
    out[1024:1280] = t[:256]
    out[1280:, :256] = t[256:384, 256:]
    out[1280:, 256:] = t[384:, 256:]


def pack_set(v, t):
    return call(pack_set_body, shape(SET_ROWS, PANEL), 0, 6 << 20, 10)(v, t)


def leaf_near_body(own, after, before, trailing, out):
    vt = split(jnp.concatenate([s[:1024].T for s in (own, after, before)], 0))
    for j in range(4):
        part = slice(j * 256, (j + 1) * 256)
        out[:, part] = dot3(vt, split(trailing[:, part]))


def leaf_near(own, after, before, trailing):
    return call(leaf_near_body, shape(384, 1024), 3 * 805306368, 7 << 20, 20)(
        own, after, before, trailing
    )


def leaf_top_body(near, own, after, before, far_a, far_b, trailing, w_out, keep, send, projected):
    y = lax.axis_index("cols")
    core = place()[0]
    vt = split(jnp.concatenate([far_a[...].T, far_b[:256].T], 1))
    rows = lax.broadcasted_iota(jnp.int32, (PANEL, 128), 0)
    cols = lax.broadcasted_iota(jnp.int32, (PANEL, 128), 1)
    factors = []
    for k, s in enumerate((own, after, far_b, before)):
        block = s[256:] if k == 2 else s[1024:]
        factors.append(jnp.where(rows <= cols + ((y + k) % 4) * 128, block, 0.0).T)
    factor = split(jnp.concatenate(factors, 0))
    tops = split(jnp.concatenate([own[:512], after[:512], far_a[:512], before[:512]], 1))
    for j in range(4):
        part = slice(j * 256, (j + 1) * 256)
        for i, k in enumerate((0, 1, 3)):
            projected[(y + k) % 4] = near[i * 128 : (i + 1) * 128, part]
        projected[(y + 2) % 4] = dot3(vt, split(trailing[:, part]))
        weight = dot3(factor, split(projected[...].reshape(PANEL, 256)))
        w_out[:, part] = weight
        top = trailing[:PANEL, part] - dot3(tops, split(weight))
        to = slice((j % 2) * 256, (j % 2 + 1) * 256)

        @pl.when(core == j // 2)
        def _():
            keep[:, to] = top

        @pl.when(core != j // 2)
        def _():
            send[:, to] = top


def leaf_top(near, own, after, before, far_a, far_b, trailing):
    return call(
        leaf_top_body,
        (shape(512, 1024), shape(512, 512), shape(512, 512)),
        3 * 1342177280,
        14 << 20,
        28,
        scratch_shapes=[pltpu.VMEM((4, 128, 256), F32)],
    )(near, own, after, before, far_a, far_b, trailing)


def leaf_rest_body(weight, own, after, before, far_a, far_b, trailing, out):
    far = jnp.concatenate([far_a[512:], far_b[:256]], 0)
    vectors = split(jnp.concatenate([own[512:1024], after[512:1024], far, before[512:1024]], 1))
    for j in range(4):
        part = slice(j * 256, (j + 1) * 256)
        out[:, part] = trailing[:, part] - dot3(vectors, split(weight[:, part]))


def leaf_rest(weight, own, after, before, far_a, far_b, trailing):
    bottom = pl.BlockSpec((512, 1024), lambda i: (1, 0))

    def whole(a):
        return pl.BlockSpec(a.shape, lambda i: (0, 0))

    args = (weight, own, after, before, far_a, far_b)
    return call(
        leaf_rest_body,
        shape(1024, 1024),
        3 * 536870912,
        10 << 20,
        28,
        grid=(1,),
        in_specs=[whole(a) for a in args] + [bottom],
        out_specs=bottom,
    )(*args, trailing)


SETS = (
    shape(5, 1024, 512, dtype=BF16),
    shape(5, 1024, 512, dtype=BF16),
    shape(5, 512, 1024, dtype=BF16),
    shape(5, 512, 1024, dtype=BF16),
)
SET_SCRATCH = [
    pltpu.VMEM((1024, 512), BF16),
    pltpu.VMEM((1024, 512), BF16),
    pltpu.VMEM((512, 1024), BF16),
    pltpu.VMEM((512, 1024), BF16),
]


def prep_body(slot, count, *refs):
    sources, refs = refs[:count], refs[count:]
    outs, held, (block, in_sem, out_sem) = refs[-11:-7], refs[-7:-3], refs[-3:]
    core, z, _ = place()
    if slot == 4:
        mine, other = sources

        @pl.when(core == 1)
        def _():
            pltpu.make_async_copy(mine, block, in_sem.at[0]).start()

        @pl.when(core != 1)
        def _():
            pltpu.make_async_copy(other, block, in_sem.at[0]).start()

        pltpu.make_async_copy(mine, block, in_sem.at[0]).wait()
        index = 4
    else:
        if slot == 0:
            mine, other = sources

            @pl.when(core == 0)
            def _():
                pltpu.make_async_copy(mine, block, in_sem.at[0]).start()

            @pl.when(core != 0)
            def _():
                pltpu.make_async_copy(other, block, in_sem.at[0]).start()

            pltpu.make_async_copy(mine, block, in_sem.at[0]).wait()
        else:
            direct, relayed = sources[: count // 2], sources[count // 2 :]
            size = SET_ROWS // (count // 2)

            def copies(refs):
                return [
                    pltpu.make_async_copy(ref, block.at[pl.ds(i * size, size)], in_sem.at[i])
                    for i, ref in enumerate(refs)
                ]

            @pl.when(core == 0)
            def _():
                for copy in copies(direct):
                    copy.start()

            @pl.when(core != 0)
            def _():
                for copy in copies(relayed):
                    copy.start()

            for copy in copies(direct):
                copy.wait()
        index = (z + slot) % 4
    ab_high, ab_low, wt_high, wt_low = held
    rows = lax.broadcasted_iota(jnp.int32, (256, 512), 0)
    cols = lax.broadcasted_iota(jnp.int32, (256, 512), 1)
    upper = split(jnp.where(rows <= cols, block[1024:1280], 0.0))
    corner = jnp.concatenate([block[1280:, :256], block[1280:, 256:]], 0)
    corner = split(jnp.where(rows[:, :256] <= cols[:, :256], corner, 0.0))
    for i in range(4):
        part = slice(i * 256, (i + 1) * 256)
        high, low = split(block[part])
        ab_high[part], ab_low[part] = high, low
        product = dot3((high[:, :256], low[:, :256]), upper)
        right = product[:, 256:] + dot3((high[:, 256:], low[:, 256:]), corner)
        wt_high[:256, part], wt_low[:256, part] = split(product[:, :256].T)
        wt_high[256:, part], wt_low[256:, part] = split(right.T)
    copies = [
        pltpu.make_async_copy(src, dst.at[index], out_sem.at[i])
        for i, (src, dst) in enumerate(zip(held, outs))
    ]
    for copy in copies:
        copy.start()
    for copy in copies:
        copy.wait()


def prep(slot, sources, sets=None):
    count = len(sources)
    sets = () if sets is None else tuple(sets)
    return call(
        functools.partial(prep_body, slot, count),
        SETS,
        3 * 2 * 1024 * 512 * 384,
        7 << 20,
        16,
        in_specs=[ANY] * (count + len(sets)),
        out_specs=(ANY,) * 4,
        input_output_aliases={count + i: i for i in range(len(sets))},
        scratch_shapes=SET_SCRATCH
        + [
            pltpu.VMEM((SET_ROWS, PANEL), F32),
            pltpu.SemaphoreType.DMA((2,)),
            pltpu.SemaphoreType.DMA((4,)),
        ],
    )(*sources, *sets)


def fetch(sets, held, index, sem):
    copies = [
        pltpu.make_async_copy(src.at[index], dst, sem.at[i])
        for i, (src, dst) in enumerate(zip(sets, held))
    ]
    for copy in copies:
        copy.start()
    return copies


def apply(held, low, up):
    ab_high, ab_low, wt_high, wt_low = held
    (low_h, low_l), (up_h, up_l) = split(low), split(up)
    high = jnp.concatenate([low_h, up_h], 0)
    rest = jnp.concatenate([low_l, up_l], 0)
    weight = split(dot3((wt_high[...], wt_low[...]), (high, rest)))
    low = low - dot3((ab_high[:512], ab_low[:512]), weight)
    up = up - dot3((ab_high[512:], ab_low[512:]), weight)
    return low, up


def merge_core_body(keep, got, s0, s1, s2, s3, o0, o1, o2, o3, up_out, h0, h1, h2, h3, low_v, sem):
    core, z, _ = place()
    held = (h0, h1, h2, h3)
    copies = fetch((s0, s1, s2, s3), held, 4, sem)
    first = core == 0
    low = jnp.where(first, keep[...], got[...])
    up = jnp.where(first, got[...], keep[...])
    for copy in copies:
        copy.wait()
    low, up_out[...] = apply(held, low, up)
    for q in range(4):
        low_v[q] = low[:, q * 128 : (q + 1) * 128]
    for k, out in enumerate((o0, o1, o2, o3)):
        out[...] = low_v[(z + k) % 4]


def merge_core(keep, got, sets):
    piece = shape(512, 128)
    return call(
        merge_core_body,
        (piece, piece, piece, piece, shape(512, 512)),
        3 * 2 * 1024 * 512 * 1024,
        8 << 20,
        24,
        in_specs=[VMEM] * 2 + [ANY] * 4,
        out_specs=(VMEM,) * 5,
        scratch_shapes=SET_SCRATCH + [pltpu.VMEM((4, 512, 128), F32), pltpu.SemaphoreType.DMA((4,))],
    )(keep, got, *sets)


def merge_z_body(g0, g1, g2, g3, s0, s1, s2, s3, low_out, r0, r1, r2, r3, *scratch):
    _, z, _ = place()
    sets = (s0, s1, s2, s3)
    held = [scratch[4 * i : 4 * i + 4] for i in range(3)]
    tops, sem = scratch[12:]
    waits = [fetch(sets, held[i], index, sem.at[i]) for i, index in enumerate((1, 3, 2))]
    for k, got in enumerate((g0, g1, g2, g3)):
        tops[(z + 4 - k) % 4] = got[...]
    for i, (a, b) in enumerate(((0, 1), (2, 3), (0, 2))):
        for copy in waits[i]:
            copy.wait()
        low, up = apply(held[i], tops[a], tops[b])
        tops[a] = low
        tops[b] = up
    low_out[...] = tops[0]
    for k, out in enumerate((r0, r1, r2, r3)):
        out[...] = tops[(z + k) % 4]


def merge_z(parts, sets):
    piece = shape(512, 128)
    return call(
        merge_z_body,
        (piece,) * 5,
        3 * 3 * 2 * 1024 * 512 * 256,
        14 << 20,
        24,
        in_specs=[VMEM] * 4 + [ANY] * 4,
        out_specs=(VMEM,) * 5,
        scratch_shapes=SET_SCRATCH * 3
        + [pltpu.VMEM((4, 512, 128), F32), pltpu.SemaphoreType.DMA((3, 4))],
    )(*parts, *sets)


def merge_x_body(low, up, s0, s1, s2, s3, low_out, up_out, h0, h1, h2, h3, sem):
    held = (h0, h1, h2, h3)
    for copy in fetch((s0, s1, s2, s3), held, 0, sem):
        copy.wait()
    low_out[...], up_out[...] = apply(held, low[...], up[...])


def merge_x(low, up, sets):
    piece = shape(512, 128)
    return call(
        merge_x_body,
        (piece, piece),
        3 * 2 * 1024 * 512 * 256,
        5 << 20,
        12,
        in_specs=[VMEM] * 2 + [ANY] * 4,
        out_specs=(VMEM,) * 2,
        scratch_shapes=SET_SCRATCH + [pltpu.SemaphoreType.DMA((4,))],
    )(low, up, *sets)


def join_body(final, r0, e1, e2, e3, l1, l2, l3, out):
    _, z, _ = place()

    def put(source, k):
        out[:, pl.ds(pl.multiple_of(((z + 4 - k) % 4) * 128, 128), 128)] = source[...]

    @pl.when(z == 0)
    def _():
        for k, source in enumerate((final, l1, l2, l3)):
            put(source, k)

    @pl.when(z != 0)
    def _():
        for k, source in enumerate((r0, e1, e2, e3)):
            put(source, k)


def join(*parts):
    return call(join_body, shape(512, 512), 0, 4 << 20, 6)(*parts)


def finish_body(half, got_half, up, got_up, rest, out, sem):
    core = place()[0]

    def copies(left, right):
        return [
            pltpu.make_async_copy(left, out.at[pl.ds(0, 512), pl.ds(0, 512)], sem.at[0]),
            pltpu.make_async_copy(right, out.at[pl.ds(0, 512), pl.ds(512, 512)], sem.at[1]),
        ]

    @pl.when(core == 0)
    def _():
        for copy in copies(half, got_half):
            copy.start()

    @pl.when(core != 0)
    def _():
        for copy in copies(got_up, up):
            copy.start()

    for copy in copies(half, got_half):
        copy.wait()


def finish(half, got_half, up, got_up, rest):
    return call(
        finish_body,
        shape(1024, 1024),
        0,
        6 << 20,
        6,
        in_specs=[VMEM] * 4 + [ANY],
        out_specs=ANY,
        input_output_aliases={4: 0},
        scratch_shapes=[pltpu.SemaphoreType.DMA((2,))],
    )(half, got_half, up, got_up, rest)


def on_device(trailing, leaf_v, leaf_t, merge_v, merge_t):
    _, z, x = place()
    own = pack_leaf(leaf_v, leaf_t)
    before = turn(own, 1)
    after = turn(own, -1)
    merge_v, merge_t = lax.optimization_barrier((merge_v, merge_t, own))[:2]
    mine = pack_set(merge_v, merge_t)
    set_below = move(mine, Z_UP_0)
    set_above = move(mine, Z_DOWN_0)
    other = move(mine, SWAP_CORE)

    far_a = turn(before[:768], 1)
    far_b = turn(after[768:], -1)
    near = leaf_near(own, after, before, trailing)
    weight, keep, send = leaf_top(near, own, after, before, far_a, far_b, trailing)
    got = move(send, SWAP_CORE)

    sets = prep(4, (behind(mine, near), other))
    sets = prep(0, (mine, other), sets)
    set_below, set_above = lax.optimization_barrier((set_below, set_above, send))[:2]
    far_up = move(set_below[:704], Z_UP_0)
    far_down = move(set_above[704:], Z_DOWN_0)
    below_1 = move(set_below, CORE_UP)
    above_1 = move(set_above, CORE_UP)
    rest = leaf_rest(weight, own, after, before, far_a, far_b, trailing)

    *parts, up0 = merge_core(keep, got, sets)
    parts = [parts[0]] + [move(parts[k], Z_TURN[k]) for k in (1, 2, 3)]
    far_up, far_down = lax.optimization_barrier((far_up, far_down, up0))[:2]
    far_up_1 = move(far_up, CORE_UP)
    far_down_1 = move(far_down, CORE_UP)
    sets = prep(1, (behind(set_above, up0), above_1), sets)
    sets = prep(3, (set_below, below_1), sets)
    sets = prep(2, (far_up, far_down, far_up_1, far_down_1), sets)
    got_up0 = move(behind(up0, *sets), CORE_UP)

    low2, r0, *returns = merge_z(parts, sets)
    from_even = move(low2, X_UP)
    early = [move(behind(returns[k - 1], from_even), Z_EARLY[k]) for k in (1, 2, 3)]
    low3, up3 = merge_x(from_even, low2, sets)
    low4, up4 = merge_x(move(low3, X_ONE_TWO), move(low3, X_THREE_TWO), sets)
    home = move(low4, X_HOME)
    final = jnp.where(x == 0, home, jnp.where(x == 2, up4, up3))
    late = [move(final, Z_LATE[k]) for k in (1, 2, 3)]
    half = join(final, r0, *early, *late)
    got_half = move(half, CORE_DOWN)
    return finish(half, got_half, up0, got_up0, rest)


def solution(mesh):
    return jax.shard_map(
        on_device,
        mesh=mesh,
        in_specs=(
            P("rows", "cols"),
            P("rows", "cols"),
            P("rows", "cols"),
            P("rows", None),
            P("rows", None),
        ),
        out_specs=P("rows", "cols"),
        check_vma=False,
    )
```

```python
import functools

import jax
import jax.numpy as jnp
from jax import lax
from jax.experimental import pallas as pl
from jax.experimental.pallas import tpu as pltpu
from jax.sharding import PartitionSpec as P


F32 = jnp.float32
BF16 = jnp.bfloat16
PANEL = 512
SET_ROWS = 1408
ANY = pl.BlockSpec(memory_space=pl.ANY)
VMEM = pl.BlockSpec(memory_space=pltpu.VMEM)


def route(pick):
    pairs = []
    for r in range(32):
        c, z, x = r & 1, (r >> 1) & 3, r >> 3
        to = pick(c, z, x)
        if to is not None:
            c, z, x = to
            pairs.append((r, (x % 4) * 8 + (z % 4) * 2 + c))
    return pairs


SWAP_CORE = route(lambda c, z, x: (1 - c, z, x))
DOWN_ACROSS = route(lambda c, z, x: (1, z - 1, x) if c == 0 else None)
Z_DOWN_1 = route(lambda c, z, x: (1, z - 1, x) if c == 1 else None)
CORE_UP = route(lambda c, z, x: (1, z, x) if c == 0 else None)
CORE_DOWN = route(lambda c, z, x: (0, z, x) if c == 1 else None)
Z_UP_0 = route(lambda c, z, x: (c, z + 1, x) if c == 0 else None)
Z_TURN = {k: route(lambda c, z, x: (c, z + k, x)) for k in (1, 2, 3)}
Z_EARLY = {k: route(lambda c, z, x: (c, z + k, x) if (z + k) % 4 else None) for k in (1, 2, 3)}
Z_LATE = {k: route(lambda c, z, x: (c, 0, x) if x and (z + k) % 4 == 0 else None) for k in (1, 2, 3)}
X_UP = route(lambda c, z, x: (c, z, x + 1) if x % 2 == 0 else None)
X_ONE_TWO = route(lambda c, z, x: (c, z, 2) if x == 1 else None)
X_THREE_TWO = route(lambda c, z, x: (c, z, 2) if x == 3 else None)
X_HOME = {k: route(lambda c, z, x: (c, 0, 0) if x == 2 and (z + k) % 4 == 0 else None) for k in range(4)}


def move(block, pairs):
    return lax.ppermute(block, "rows", pairs)


def turn(block, by):
    count = lax.axis_size("cols")
    return lax.ppermute(block, "cols", [(i, (i + by) % count) for i in range(count)])


def split(block):
    high = block.astype(BF16)
    return high, (block - high.astype(F32)).astype(BF16)


def dot(left, right):
    return jnp.dot(left, right, preferred_element_type=F32)


def dot3(left, right):
    (lh, ll), (rh, rl) = left, right
    return dot(lh, rh) + (dot(lh, rl) + dot(ll, rh))


def dot_tall(left, right):
    (lh, ll), (rh, rl) = left, right
    n = lh.shape[0]
    both = dot(jnp.concatenate([lh, ll], 0), rh)
    return both[:n] + (both[n:] + dot(lh, rl))


def place():
    me = lax.axis_index("rows")
    return me % 2, (me // 2) % 4, me // 8


def shape(*dims, dtype=F32):
    return jax.ShapeDtypeStruct(dims, dtype)


def call(body, outs, flops, moved, mib, **options):
    return pl.pallas_call(
        body,
        out_shape=outs,
        cost_estimate=pl.CostEstimate(flops=flops, bytes_accessed=moved, transcendentals=0),
        compiler_params=pltpu.CompilerParams(vmem_limit_bytes=mib << 20),
        **options,
    )


def copy_all(sem, *pairs):
    copies = [pltpu.make_async_copy(src, dst, sem.at[i]) for i, (src, dst) in enumerate(pairs)]
    for copy in copies:
        copy.start()
    for copy in copies:
        copy.wait()


def pack_leaf_body(v, t, first, second, sem):
    copy_all(
        sem,
        (v.at[pl.ds(0, 768)], first),
        (v.at[pl.ds(768, 256)], second.at[pl.ds(0, 256)]),
        (t, second.at[pl.ds(256, 512)]),
    )


def pack_leaf(v, t):
    outs = (shape(768, 128), shape(768, 128))
    return call(
        pack_leaf_body,
        outs,
        0,
        3 << 19,
        1,
        in_specs=[ANY] * 2,
        out_specs=(VMEM,) * 2,
        scratch_shapes=[pltpu.SemaphoreType.DMA((3,))],
    )(v, t)


def pack_set_body(v, t, first, second, sem):
    copy_all(
        sem,
        (v.at[pl.ds(0, 704)], first),
        (v.at[pl.ds(704, 320)], second.at[pl.ds(0, 320)]),
        (t.at[pl.ds(0, 256)], second.at[pl.ds(320, 256)]),
        (t.at[pl.ds(256, 128), pl.ds(256, 256)], second.at[pl.ds(576, 128), pl.ds(0, 256)]),
        (t.at[pl.ds(384, 128), pl.ds(256, 256)], second.at[pl.ds(576, 128), pl.ds(256, 256)]),
    )


def pack_set(v, t):
    outs = (shape(704, PANEL), shape(704, PANEL))
    return call(
        pack_set_body,
        outs,
        0,
        6 << 20,
        1,
        in_specs=[ANY] * 2,
        out_specs=(VMEM,) * 2,
        scratch_shapes=[pltpu.SemaphoreType.DMA((5,))],
    )(v, t)


def masked(second, offset):
    rows = lax.broadcasted_iota(jnp.int32, (PANEL, 128), 0)
    cols = lax.broadcasted_iota(jnp.int32, (PANEL, 128), 1)
    return jnp.where(rows <= cols + offset * 128, second[256:], 0.0).T


def leaf_near_body(
    a0, b0, a1, b1, a3, b3, trailing, c_high, c_low, p_high, p_low, f_high, f_low, v_high, v_low, w_near, c_top
):
    c_top[...] = trailing[:PANEL]
    y = lax.axis_index("cols")
    slots = (0, 1, 3)
    shards = ((a0, b0), (a1, b1), (a3, b3))
    vt = [jnp.concatenate([a[...].T, b[:256].T], 1) for a, b in shards]
    vt = split(jnp.concatenate(vt, 0))
    for i, (k, (a, b)) in enumerate(zip(slots, shards)):
        part = slice(i * 128, (i + 1) * 128)
        f_high[part], f_low[part] = split(masked(b, (y + k) % 4))
        v_high[:, part], v_low[:, part] = split(a[:512])
    p_high[(y + 2) % 4] = jnp.zeros((128, 1024), BF16)
    p_low[(y + 2) % 4] = jnp.zeros((128, 1024), BF16)
    for j in range(4):
        part = slice(j * 256, (j + 1) * 256)
        c = split(trailing[:, part])
        c_high[:, part], c_low[:, part] = c
        p = split(dot3(vt, c))
        for i, k in enumerate(slots):
            at = slice(i * 128, (i + 1) * 128)
            p_high[(y + k) % 4, :, part] = p[0][at]
            p_low[(y + k) % 4, :, part] = p[1][at]
        p = [q[:, :, part].reshape(PANEL, 256) for q in (p_high, p_low)]
        w_near[:, part] = dot3((f_high[...], f_low[...]), p)


def leaf_near(own, after, before, trailing):
    outs = (
        *[shape(1024, 1024, dtype=BF16)] * 2,
        *[shape(4, 128, 1024, dtype=BF16)] * 2,
        *[shape(384, 512, dtype=BF16)] * 2,
        *[shape(512, 384, dtype=BF16)] * 2,
        shape(384, 1024),
        shape(512, 1024),
    )
    return call(leaf_near_body, outs, 3 * 1200000000, 7 << 20, 12)(*own, *after, *before, trailing)


def leaf_top_body(
    c_high, c_low, p_high, p_low, f_high, f_low, v_high, v_low, w_near, c_top, a2, b2, w_out, keep, send
):
    far = (lax.axis_index("cols") + 2) % 4
    core = place()[0]
    vt = split(jnp.concatenate([a2[...].T, b2[:256].T], 1))
    factor = split(masked(b2, far))
    lanes = pl.ds(pl.multiple_of(far * 128, 128), 128)
    near_far = f_high[:, lanes], f_low[:, lanes]
    v_far = split(a2[:512])
    for j in range(4):
        part = slice(j * 256, (j + 1) * 256)
        p_far = split(dot_tall(vt, (c_high[:, part], c_low[:, part])))
        p_high[far, :, part], p_low[far, :, part] = p_far
        p = [q[:, :, part].reshape(PANEL, 256) for q in (p_high, p_low)]
        w0 = w_near[:, part] + dot3(near_far, p_far)
        w1 = dot_tall(factor, p)
        w_out[:384, part] = w0
        w_out[384:, part] = w1
        top = c_top[:, part] - (dot3((v_high[...], v_low[...]), split(w0)) + dot3(v_far, split(w1)))
        to = slice((j % 2) * 256, (j % 2 + 1) * 256)

        @pl.when(core == j // 2)
        def _():
            keep[:, to] = top

        @pl.when(core != j // 2)
        def _():
            send[:, to] = top


def leaf_top(near, far):
    outs = (shape(512, 1024), shape(512, 512), shape(512, 512))
    return call(leaf_top_body, outs, 3 * 1000000000, 14 << 20, 12)(*near, *far)


def leaf_rest_body(weight, a0, b0, a1, b1, a3, b3, a2, b2, trailing, out):
    shards = ((a0, b0), (a1, b1), (a3, b3), (a2, b2))
    vectors = [jnp.concatenate([a[512:], b[:256]], 0) for a, b in shards]
    vectors = split(jnp.concatenate(vectors, 1))
    for j in range(4):
        part = slice(j * 256, (j + 1) * 256)
        out[:, part] = trailing[:, part] - dot3(vectors, split(weight[:, part]))


def leaf_rest(weight, own, after, before, far, trailing):
    bottom = pl.BlockSpec((512, 1024), lambda i: (1, 0))

    def whole(a):
        return pl.BlockSpec(a.shape, lambda i: (0, 0))

    args = (weight, *own, *after, *before, *far)
    return call(
        leaf_rest_body,
        shape(1024, 1024),
        3 * 536870912,
        10 << 20,
        20,
        grid=(1,),
        in_specs=[whole(a) for a in args] + [bottom],
        out_specs=bottom,
    )(*args, trailing)


SETS = (
    shape(5, 1024, 512, dtype=BF16),
    shape(5, 1024, 512, dtype=BF16),
    shape(5, 512, 1024, dtype=BF16),
    shape(5, 512, 1024, dtype=BF16),
)


def prep_body(slot, *refs):
    (a0, b0, a1, b1), refs = refs[:4], refs[4:]
    ab_high, ab_low, wt_high, wt_low, block, sem = refs[-6:]
    core, z, _ = place()

    def copies(first, second):
        half = SET_ROWS // 2
        return [
            pltpu.make_async_copy(first, block.at[pl.ds(0, half)], sem.at[0]),
            pltpu.make_async_copy(second, block.at[pl.ds(half, half)], sem.at[1]),
        ]

    on_core = 1 if slot == 4 else 0

    @pl.when(core == on_core)
    def _():
        for copy in copies(a0, b0):
            copy.start()

    @pl.when(core != on_core)
    def _():
        for copy in copies(a1, b1):
            copy.start()

    for copy in copies(a0, b0):
        copy.wait()
    index = 4 if slot == 4 else (z + slot) % 4
    rows = lax.broadcasted_iota(jnp.int32, (256, 512), 0)
    cols = lax.broadcasted_iota(jnp.int32, (256, 512), 1)
    upper = split(jnp.where(rows <= cols, block[1024:1280], 0.0))
    corner = jnp.concatenate([block[1280:, :256], block[1280:, 256:]], 0)
    corner = split(jnp.where(rows[:, :256] <= cols[:, :256], corner, 0.0))
    for i in range(4):
        part = slice(i * 256, (i + 1) * 256)
        high, low = split(block[part])
        ab_high[index, part], ab_low[index, part] = high, low
        product = dot3((high[:, :256], low[:, :256]), upper)
        right = product[:, 256:] + dot3((high[:, 256:], low[:, 256:]), corner)
        wt_high[index, :256, part], wt_low[index, :256, part] = split(product[:, :256].T)
        wt_high[index, 256:, part], wt_low[index, 256:, part] = split(right.T)


def prep(slot, on_core, off_core, sets=()):
    return call(
        functools.partial(prep_body, slot),
        SETS,
        3 * 2 * 1024 * 512 * 384,
        7 << 20,
        10,
        in_specs=[ANY] * 4 + [VMEM] * len(sets),
        out_specs=(VMEM,) * 4,
        input_output_aliases={4 + i: i for i in range(len(sets))},
        scratch_shapes=[pltpu.VMEM((SET_ROWS, PANEL), F32), pltpu.SemaphoreType.DMA((2,))],
    )(*on_core, *off_core, *sets)


def dot_wide(left, right):
    (lh, ll), (rh, rl) = left, right
    n = rh.shape[1]
    if n > 128:
        return dot3(left, right)
    both = dot(lh, jnp.concatenate([rh, rl], 1))
    return both[:, :n] + (both[:, n:] + dot(ll, rh))


def apply(sets, index, low, up):
    ab_high, ab_low, wt_high, wt_low = sets
    (low_h, low_l), (up_h, up_l) = split(low), split(up)
    tops = jnp.concatenate([low_h, up_h], 0), jnp.concatenate([low_l, up_l], 0)
    weight = split(dot_wide((wt_high[index], wt_low[index]), tops))
    low = low - dot_wide((ab_high[index, :512], ab_low[index, :512]), weight)
    up = up - dot_wide((ab_high[index, 512:], ab_low[index, 512:]), weight)
    return low, up


def merge_core_body(keep, got, s0, s1, s2, s3, o0, o1, o2, o3, up_out, low_v):
    core, z, _ = place()
    first = core == 0
    low = jnp.where(first, keep[...], got[...])
    up = jnp.where(first, got[...], keep[...])
    low, up_out[...] = apply((s0, s1, s2, s3), 4, low, up)
    for q in range(4):
        low_v[q] = low[:, q * 128 : (q + 1) * 128]
    for k, out in enumerate((o0, o1, o2, o3)):
        out[...] = low_v[(z + k) % 4]


PIECE = shape(512, 128)


def merge_core(keep, got, sets):
    return call(
        merge_core_body,
        (*[PIECE] * 4, shape(512, 512)),
        3 * 2 * 1024 * 512 * 1024,
        8 << 20,
        8,
        scratch_shapes=[pltpu.VMEM((4, 512, 128), F32)],
    )(keep, got, *sets)


def merge_z_body(g0, g1, g2, g3, s0, s1, s2, s3, low_out, r0, r1, r2, r3, tops):
    _, z, _ = place()
    for k, got in enumerate((g0, g1, g2, g3)):
        tops[(z + 4 - k) % 4] = got[...]
    for index, a, b in ((1, 0, 1), (3, 2, 3), (2, 0, 2)):
        tops[a], tops[b] = apply((s0, s1, s2, s3), index, tops[a], tops[b])
    low_out[...] = tops[0]
    for k, out in enumerate((r0, r1, r2, r3)):
        out[...] = tops[(z + k) % 4]


def merge_z(parts, sets):
    return call(
        merge_z_body,
        (PIECE,) * 5,
        3 * 3 * 2 * 1024 * 512 * 256,
        14 << 20,
        4,
        scratch_shapes=[pltpu.VMEM((4, 512, 128), F32)],
    )(*parts, *sets)


def merge_x3_body(low, up, s0, s1, s2, s3, low_out, up_out):
    low_out[...], up_out[...] = apply((s0, s1, s2, s3), 0, low[...], up[...])


def merge_x4_body(low, up, up3, s0, s1, s2, s3, low_out, own_out):
    low_out[...], up4 = apply((s0, s1, s2, s3), 0, low[...], up[...])
    own_out[...] = jnp.where(place()[2] == 2, up4, up3[...])


def merge_x(body, *args):
    return call(body, (PIECE, PIECE), 3 * 2 * 1024 * 512 * 256, 5 << 20, 3)(*args)


def join_body(own, r0, e1, e2, e3, l1, l2, l3, h0, h1, h2, h3, out):
    _, z, x = place()

    def put(parts):
        for k, source in enumerate(parts):
            out[:, pl.ds(pl.multiple_of(((z + 4 - k) % 4) * 128, 128), 128)] = source[...]

    @pl.when(z != 0)
    def _():
        put((r0, e1, e2, e3))

    @pl.when((z == 0) & (x != 0))
    def _():
        put((own, l1, l2, l3))

    @pl.when((z == 0) & (x == 0))
    def _():
        put((h0, h1, h2, h3))


def join(*parts):
    return call(join_body, shape(512, 512), 0, 4 << 20, 1)(*parts)


def finish_body(half, got_half, up, got_up, rest, out, sem):
    core = place()[0]

    def copies(left, right):
        return [
            pltpu.make_async_copy(left, out.at[pl.ds(0, 512), pl.ds(0, 512)], sem.at[0]),
            pltpu.make_async_copy(right, out.at[pl.ds(0, 512), pl.ds(512, 512)], sem.at[1]),
        ]

    @pl.when(core == 0)
    def _():
        for copy in copies(half, got_half):
            copy.start()

    @pl.when(core != 0)
    def _():
        for copy in copies(got_up, up):
            copy.start()

    for copy in copies(half, got_half):
        copy.wait()


def finish(half, got_half, up, got_up, rest):
    return call(
        finish_body,
        shape(1024, 1024),
        0,
        6 << 20,
        6,
        in_specs=[VMEM] * 4 + [ANY],
        out_specs=ANY,
        input_output_aliases={4: 0},
        scratch_shapes=[pltpu.SemaphoreType.DMA((2,))],
    )(half, got_half, up, got_up, rest)


def on_device(trailing, leaf_v, leaf_t, merge_v, merge_t):
    own_a, own_b = pack_leaf(leaf_v, leaf_t)
    before_a = turn(own_a, 1)
    after_b = turn(own_b, -1)
    before_b = turn(own_b, 1)
    after_a = turn(own_a, -1)
    far = turn(before_a, 1), turn(after_b, -1)
    own, after, before = (own_a, own_b), (after_a, after_b), (before_a, before_b)

    mine = pack_set(merge_v, merge_t)
    below_a = move(mine[0], Z_UP_0)
    above_b = move(mine[1], DOWN_ACROSS)
    below_b = move(mine[1], Z_UP_0)
    above_a = move(mine[0], DOWN_ACROSS)
    other = move(mine[0], SWAP_CORE), move(mine[1], SWAP_CORE)
    far_a = move(below_a, Z_UP_0)
    far_b = move(above_b, Z_DOWN_1)
    below_1 = move(below_a, CORE_UP), move(below_b, CORE_UP)
    above_0 = move(above_a, CORE_DOWN), move(above_b, CORE_DOWN)
    far_a_1 = move(far_a, CORE_UP)
    far_b_0 = move(far_b, CORE_DOWN)

    sets = prep(4, mine, other)
    near = leaf_near(own, after, before, trailing)
    weight, keep, send = leaf_top(near, far)
    got = move(send, SWAP_CORE)
    *parts, up0 = merge_core(keep, got, sets)
    sets = lax.optimization_barrier((*sets, up0))[:4]
    sets = prep(0, mine, other, sets)
    parts = [parts[0]] + [move(parts[k], Z_TURN[k]) for k in (1, 2, 3)]
    sets = prep(3, (below_a, below_b), below_1, sets)
    sets = prep(1, above_0, (above_a, above_b), sets)
    sets = prep(2, (far_a, far_b_0), (far_a_1, far_b), sets)
    rest = leaf_rest(weight, own, after, before, far, trailing)

    low2, r0, *returns = merge_z(parts, sets)
    from_even = move(low2, X_UP)
    early = [move(returns[k - 1], Z_EARLY[k]) for k in (1, 2, 3)]
    got_up0 = move(up0, CORE_UP)
    low3, up3 = merge_x(merge_x3_body, from_even, low2, *sets)
    from_one = move(low3, X_ONE_TWO)
    from_three = move(low3, X_THREE_TWO)
    low4, own_top = merge_x(merge_x4_body, from_one, from_three, up3, *sets)
    home = [move(low4, X_HOME[k]) for k in range(4)]
    late = [move(own_top, Z_LATE[k]) for k in (1, 2, 3)]
    half = join(own_top, r0, *early, *late, *home)
    got_half = move(half, CORE_DOWN)
    return finish(half, got_half, up0, got_up0, rest)


def solution(mesh):
    return jax.shard_map(
        on_device,
        mesh=mesh,
        in_specs=(
            P("rows", "cols"),
            P("rows", "cols"),
            P("rows", "cols"),
            P("rows", None),
            P("rows", None),
        ),
        out_specs=P("rows", "cols"),
        check_vma=False,
    )
```

```python
import functools

import jax
import jax.numpy as jnp
from jax import lax
from jax.experimental import pallas as pl
from jax.experimental.pallas import tpu as pltpu
from jax.sharding import PartitionSpec as P


F32 = jnp.float32
BF16 = jnp.bfloat16
PANEL = 512
SET_ROWS = 1408
ANY = pl.BlockSpec(memory_space=pl.ANY)
VMEM = pl.BlockSpec(memory_space=pltpu.VMEM)


def route(pick):
    pairs = []
    for r in range(32):
        c, z, x = r & 1, (r >> 1) & 3, r >> 3
        to = pick(c, z, x)
        if to is not None:
            c, z, x = to
            pairs.append((r, (x % 4) * 8 + (z % 4) * 2 + c))
    return pairs


SWAP_CORE = route(lambda c, z, x: (1 - c, z, x))
CORE_UP = route(lambda c, z, x: (1, z, x) if c == 0 else None)
CORE_DOWN = route(lambda c, z, x: (0, z, x) if c == 1 else None)
Z_OUT = route(lambda c, z, x: (c, z - 1 if c else z + 1, x))
Z_TURN = {k: route(lambda c, z, x: (c, z + k, x)) for k in (1, 2, 3)}
Z_EARLY = {k: route(lambda c, z, x: (c, z + k, x) if (z + k) % 4 else None) for k in (1, 2, 3)}
Z_LATE = {k: route(lambda c, z, x: (c, 0, x) if x and (z + k) % 4 == 0 else None) for k in (1, 2, 3)}
X_UP = route(lambda c, z, x: (c, z, x + 1) if x % 2 == 0 else None)
X_ONE_TWO = route(lambda c, z, x: (c, z, 2) if x == 1 else None)
X_THREE_TWO = route(lambda c, z, x: (c, z, 2) if x == 3 else None)
X_HOME = {k: route(lambda c, z, x: (c, 0, 0) if x == 2 and (z + k) % 4 == 0 else None) for k in range(4)}


def move(block, pairs):
    return lax.ppermute(block, "rows", pairs)


def turn(block, by):
    count = lax.axis_size("cols")
    return lax.ppermute(block, "cols", [(i, (i + by) % count) for i in range(count)])


def split(block):
    high = block.astype(BF16)
    return high, (block - high.astype(F32)).astype(BF16)


def dot(left, right):
    return jnp.dot(left, right, preferred_element_type=F32)


def dot3(left, right):
    (lh, ll), (rh, rl) = left, right
    return dot(lh, rh) + (dot(lh, rl) + dot(ll, rh))


def dot_tall(left, right):
    (lh, ll), (rh, rl) = left, right
    n = lh.shape[0]
    both = dot(jnp.concatenate([lh, ll], 0), rh)
    return both[:n] + (both[n:] + dot(lh, rl))


def place():
    me = lax.axis_index("rows")
    return me % 2, (me // 2) % 4, me // 8


def shape(*dims, dtype=F32):
    return jax.ShapeDtypeStruct(dims, dtype)


def call(body, outs, flops, moved, mib, **options):
    return pl.pallas_call(
        body,
        out_shape=outs,
        cost_estimate=pl.CostEstimate(flops=flops, bytes_accessed=moved, transcendentals=0),
        compiler_params=pltpu.CompilerParams(vmem_limit_bytes=mib << 20),
        **options,
    )


def copy_all(sem, *pairs):
    copies = [pltpu.make_async_copy(src, dst, sem.at[i]) for i, (src, dst) in enumerate(pairs)]
    for copy in copies:
        copy.start()
    for copy in copies:
        copy.wait()


def pack_leaf_body(v, t, first, second, sem):
    copy_all(
        sem,
        (v.at[pl.ds(0, 768)], first),
        (v.at[pl.ds(768, 256)], second.at[pl.ds(0, 256)]),
        (t, second.at[pl.ds(256, 512)]),
    )


def pack_leaf(v, t):
    outs = (shape(768, 128), shape(768, 128))
    return call(
        pack_leaf_body,
        outs,
        0,
        3 << 19,
        1,
        in_specs=[ANY] * 2,
        out_specs=(VMEM,) * 2,
        scratch_shapes=[pltpu.SemaphoreType.DMA((3,))],
    )(v, t)


def pack_set_body(v, t, first, second, sem):
    copy_all(
        sem,
        (v.at[pl.ds(0, 704)], first),
        (v.at[pl.ds(704, 320)], second.at[pl.ds(0, 320)]),
        (t.at[pl.ds(0, 256)], second.at[pl.ds(320, 256)]),
        (t.at[pl.ds(256, 128), pl.ds(256, 256)], second.at[pl.ds(576, 128), pl.ds(0, 256)]),
        (t.at[pl.ds(384, 128), pl.ds(256, 256)], second.at[pl.ds(576, 128), pl.ds(256, 256)]),
    )


def pack_set(v, t):
    outs = (shape(704, PANEL), shape(704, PANEL))
    return call(
        pack_set_body,
        outs,
        0,
        6 << 20,
        1,
        in_specs=[ANY] * 2,
        out_specs=(VMEM,) * 2,
        scratch_shapes=[pltpu.SemaphoreType.DMA((5,))],
    )(v, t)


def masked(second, offset):
    rows = lax.broadcasted_iota(jnp.int32, (PANEL, 128), 0)
    cols = lax.broadcasted_iota(jnp.int32, (PANEL, 128), 1)
    return jnp.where(rows <= cols + offset * 128, second[256:], 0.0).T


def leaf_near_body(
    a0, b0, a1, b1, a3, b3, trailing, c_high, c_low, p_high, p_low, f_high, f_low, v_high, v_low, w_near, c_top
):
    c_top[...] = trailing[:PANEL]
    y = lax.axis_index("cols")
    slots = (0, 1, 3)
    shards = ((a0, b0), (a1, b1), (a3, b3))
    vt = [jnp.concatenate([a[...].T, b[:256].T], 1) for a, b in shards]
    vt = split(jnp.concatenate(vt, 0))
    for i, (k, (a, b)) in enumerate(zip(slots, shards)):
        part = slice(i * 128, (i + 1) * 128)
        f_high[part], f_low[part] = split(masked(b, (y + k) % 4))
        v_high[:, part], v_low[:, part] = split(a[:512])
    p_high[(y + 2) % 4] = jnp.zeros((128, 1024), BF16)
    p_low[(y + 2) % 4] = jnp.zeros((128, 1024), BF16)
    for j in range(4):
        part = slice(j * 256, (j + 1) * 256)
        c = split(trailing[:, part])
        c_high[:, part], c_low[:, part] = c
        p = split(dot3(vt, c))
        for i, k in enumerate(slots):
            at = slice(i * 128, (i + 1) * 128)
            p_high[(y + k) % 4, :, part] = p[0][at]
            p_low[(y + k) % 4, :, part] = p[1][at]
        p = [q[:, :, part].reshape(PANEL, 256) for q in (p_high, p_low)]
        w_near[:, part] = dot3((f_high[...], f_low[...]), p)


def leaf_near(own, after, before, trailing):
    outs = (
        *[shape(1024, 1024, dtype=BF16)] * 2,
        *[shape(4, 128, 1024, dtype=BF16)] * 2,
        *[shape(384, 512, dtype=BF16)] * 2,
        *[shape(512, 512, dtype=BF16)] * 2,
        shape(384, 1024),
        shape(512, 1024),
    )
    return call(leaf_near_body, outs, 3 * 1200000000, 7 << 20, 12)(*own, *after, *before, trailing)


def leaf_top_body(
    c_high, c_low, _0, _1, f_high, f_low, _2, _3, w_near, c_top, a2, b2,
    w_out, keep, send, p_high, p_low, v_high, v_low,
):
    far = (lax.axis_index("cols") + 2) % 4
    core = place()[0]
    vt = split(jnp.concatenate([a2[...].T, b2[:256].T], 1))
    factor = split(masked(b2, far))
    lanes = pl.ds(pl.multiple_of(far * 128, 128), 128)
    near_far = f_high[:, lanes], f_low[:, lanes]
    v_high[:, 384:], v_low[:, 384:] = split(a2[:512])
    for j in range(4):
        part = slice(j * 256, (j + 1) * 256)
        p_far = split(dot_tall(vt, (c_high[:, part], c_low[:, part])))
        p_high[far, :, part], p_low[far, :, part] = p_far
        p = [q[:, :, part].reshape(PANEL, 256) for q in (p_high, p_low)]
        near = w_near[:, part] + dot3(near_far, p_far)
        weight = jnp.concatenate([near, dot_tall(factor, p)], 0)
        w_out[:, part] = weight
        top = c_top[:, part] - dot3((v_high[...], v_low[...]), split(weight))
        to = slice((j % 2) * 256, (j % 2 + 1) * 256)

        @pl.when(core == j // 2)
        def _():
            keep[:, to] = top

        @pl.when(core != j // 2)
        def _():
            send[:, to] = top


def leaf_top(near, far):
    outs = (
        shape(512, 1024),
        *[shape(512, 512)] * 2,
        *[shape(4, 128, 1024, dtype=BF16)] * 2,
        *[shape(512, 512, dtype=BF16)] * 2,
    )
    aliases = {2: 3, 3: 4, 6: 5, 7: 6}
    return call(
        leaf_top_body, outs, 3 * 1000000000, 14 << 20, 8, input_output_aliases=aliases
    )(*near, *far)[:3]


def leaf_rest_body(weight, a0, b0, a1, b1, a3, b3, a2, b2, trailing, out):
    shards = ((a0, b0), (a1, b1), (a3, b3), (a2, b2))
    vectors = [jnp.concatenate([a[512:], b[:256]], 0) for a, b in shards]
    vectors = split(jnp.concatenate(vectors, 1))

    def step(j, carry):
        part = pl.ds(pl.multiple_of(j * 256, 256), 256)
        out[:, part] = trailing[:, part] - dot3(vectors, split(weight[:, part]))
        return carry

    lax.fori_loop(0, 4, step, 0)


def leaf_rest(weight, own, after, before, far, trailing):
    bottom = pl.BlockSpec((512, 1024), lambda i: (1, 0))

    def whole(a):
        return pl.BlockSpec(a.shape, lambda i: (0, 0))

    args = (weight, *own, *after, *before, *far)
    return call(
        leaf_rest_body,
        shape(1024, 1024),
        3 * 536870912,
        10 << 20,
        20,
        grid=(1,),
        in_specs=[whole(a) for a in args] + [bottom],
        out_specs=bottom,
    )(*args, trailing)


SETS = (
    shape(5, 1024, 512, dtype=BF16),
    shape(5, 1024, 512, dtype=BF16),
    shape(5, 512, 1024, dtype=BF16),
    shape(5, 512, 1024, dtype=BF16),
)


def pick_body(a0, b0, a1, b1, first, second, sem):
    core = place()[0]

    def copies(one, two):
        return [
            pltpu.make_async_copy(one, first, sem.at[0]),
            pltpu.make_async_copy(two, second, sem.at[1]),
        ]

    @pl.when(core == 0)
    def _():
        for copy in copies(a0, b0):
            copy.start()

    @pl.when(core != 0)
    def _():
        for copy in copies(b1, a1):
            copy.start()

    for copy in copies(a0, b0):
        copy.wait()


def pick(mine, other):
    return call(
        pick_body,
        (shape(704, PANEL),) * 2,
        0,
        6 << 20,
        1,
        in_specs=[ANY] * 4,
        out_specs=(ANY,) * 2,
        scratch_shapes=[pltpu.SemaphoreType.DMA((2,))],
    )(*mine, *other)


def prep_body(slot, *refs):
    (a0, b0, a1, b1), refs = refs[:4], refs[4:]
    ab_high, ab_low, wt_high, wt_low, block, sem = refs[-6:]
    core, z, _ = place()
    half = SET_ROWS // 2

    def copies(one, two):
        return [
            pltpu.make_async_copy(one, block.at[pl.ds(0, half)], sem.at[0]),
            pltpu.make_async_copy(two, block.at[pl.ds(half, half)], sem.at[1]),
        ]

    on_core = 1 if slot == 4 else 0

    @pl.when(core == on_core)
    def _():
        for copy in copies(a0, b0):
            copy.start()

    @pl.when(core != on_core)
    def _():
        for copy in copies(a1, b1):
            copy.start()

    for copy in copies(a0, b0):
        copy.wait()
    index = 4 if slot == 4 else (z + slot) % 4
    rows = lax.broadcasted_iota(jnp.int32, (256, 512), 0)
    cols = lax.broadcasted_iota(jnp.int32, (256, 512), 1)
    upper = split(jnp.where(rows <= cols, block[1024:1280], 0.0))
    corner = jnp.concatenate([block[1280:, :256], block[1280:, 256:]], 0)
    corner = split(jnp.where(rows[:, :256] <= cols[:, :256], corner, 0.0))

    def step(i, carry):
        part = pl.ds(pl.multiple_of(i * 256, 256), 256)
        high, low = split(block[part])
        ab_high[index, part], ab_low[index, part] = high, low
        product = dot3((high[:, :256], low[:, :256]), upper)
        right = product[:, 256:] + dot3((high[:, 256:], low[:, 256:]), corner)
        wt_high[index, :256, part], wt_low[index, :256, part] = split(product[:, :256].T)
        wt_high[index, 256:, part], wt_low[index, 256:, part] = split(right.T)
        return carry

    lax.fori_loop(0, 4, step, 0)


def prep(slot, on_core, off_core, sets=()):
    return call(
        functools.partial(prep_body, slot),
        SETS,
        3 * 2 * 1024 * 512 * 384,
        7 << 20,
        8,
        in_specs=[ANY] * 4 + [VMEM] * len(sets),
        out_specs=(VMEM,) * 4,
        input_output_aliases={4 + i: i for i in range(len(sets))},
        scratch_shapes=[pltpu.VMEM((SET_ROWS, PANEL), F32), pltpu.SemaphoreType.DMA((2,))],
    )(*on_core, *off_core, *sets)


def dot_wide(left, right):
    (lh, ll), (rh, rl) = left, right
    n = rh.shape[1]
    if n > 128:
        return dot3(left, right)
    both = dot(lh, jnp.concatenate([rh, rl], 1))
    return both[:, :n] + (both[:, n:] + dot(ll, rh))


def apply(sets, index, low, up):
    ab_high, ab_low, wt_high, wt_low = sets
    (low_h, low_l), (up_h, up_l) = split(low), split(up)
    tops = jnp.concatenate([low_h, up_h], 0), jnp.concatenate([low_l, up_l], 0)
    weight = split(dot_wide((wt_high[index], wt_low[index]), tops))
    low = low - dot_wide((ab_high[index, :512], ab_low[index, :512]), weight)
    up = up - dot_wide((ab_high[index, 512:], ab_low[index, 512:]), weight)
    return low, up


def merge_core_body(keep, got, s0, s1, s2, s3, o0, o1, o2, o3, up_out, low_v):
    core, z, _ = place()
    first = core == 0
    low = jnp.where(first, keep[...], got[...])
    up = jnp.where(first, got[...], keep[...])
    low, up_out[...] = apply((s0, s1, s2, s3), 4, low, up)
    for q in range(4):
        low_v[q] = low[:, q * 128 : (q + 1) * 128]
    for k, out in enumerate((o0, o1, o2, o3)):
        out[...] = low_v[(z + k) % 4]


PIECE = shape(512, 128)


def merge_core(keep, got, sets):
    return call(
        merge_core_body,
        (*[PIECE] * 4, shape(512, 512)),
        3 * 2 * 1024 * 512 * 1024,
        8 << 20,
        8,
        scratch_shapes=[pltpu.VMEM((4, 512, 128), F32)],
    )(keep, got, *sets)


def merge_z_body(g0, g1, g2, g3, s0, s1, s2, s3, low_out, r0, r1, r2, r3, tops):
    _, z, _ = place()
    for k, got in enumerate((g0, g1, g2, g3)):
        tops[(z + 4 - k) % 4] = got[...]
    for index, a, b in ((1, 0, 1), (3, 2, 3), (2, 0, 2)):
        tops[a], tops[b] = apply((s0, s1, s2, s3), index, tops[a], tops[b])
    low_out[...] = tops[0]
    for k, out in enumerate((r0, r1, r2, r3)):
        out[...] = tops[(z + k) % 4]


def merge_z(parts, sets):
    return call(
        merge_z_body,
        (PIECE,) * 5,
        3 * 3 * 2 * 1024 * 512 * 256,
        14 << 20,
        4,
        scratch_shapes=[pltpu.VMEM((4, 512, 128), F32)],
    )(*parts, *sets)


def merge_x3_body(low, up, s0, s1, s2, s3, low_out, up_out):
    low_out[...], up_out[...] = apply((s0, s1, s2, s3), 0, low[...], up[...])


def merge_x4_body(low, up, up3, s0, s1, s2, s3, low_out, own_out):
    low_out[...], up4 = apply((s0, s1, s2, s3), 0, low[...], up[...])
    own_out[...] = jnp.where(place()[2] == 2, up4, up3[...])


def merge_x(body, *args):
    return call(body, (PIECE, PIECE), 3 * 2 * 1024 * 512 * 256, 5 << 20, 3)(*args)


def join_body(own, r0, e1, e2, e3, l1, l2, l3, h0, h1, h2, h3, out):
    _, z, x = place()

    def put(parts):
        for k, source in enumerate(parts):
            out[:, pl.ds(pl.multiple_of(((z + 4 - k) % 4) * 128, 128), 128)] = source[...]

    @pl.when(z != 0)
    def _():
        put((r0, e1, e2, e3))

    @pl.when((z == 0) & (x != 0))
    def _():
        put((own, l1, l2, l3))

    @pl.when((z == 0) & (x == 0))
    def _():
        put((h0, h1, h2, h3))


def join(*parts):
    return call(join_body, shape(512, 512), 0, 4 << 20, 1)(*parts)


def finish_body(half, got_half, up, got_up, rest, out, sem):
    core = place()[0]

    def copies(left, right):
        return [
            pltpu.make_async_copy(left, out.at[pl.ds(0, 512), pl.ds(0, 512)], sem.at[0]),
            pltpu.make_async_copy(right, out.at[pl.ds(0, 512), pl.ds(512, 512)], sem.at[1]),
        ]

    @pl.when(core == 0)
    def _():
        for copy in copies(half, got_half):
            copy.start()

    @pl.when(core != 0)
    def _():
        for copy in copies(got_up, up):
            copy.start()

    for copy in copies(half, got_half):
        copy.wait()


def finish(half, got_half, up, got_up, rest):
    return call(
        finish_body,
        shape(1024, 1024),
        0,
        6 << 20,
        6,
        in_specs=[VMEM] * 4 + [ANY],
        out_specs=ANY,
        input_output_aliases={4: 0},
        scratch_shapes=[pltpu.SemaphoreType.DMA((2,))],
    )(half, got_half, up, got_up, rest)


def on_device(trailing, leaf_v, leaf_t, merge_v, merge_t):
    own_a, own_b = pack_leaf(leaf_v, leaf_t)
    before_a = turn(own_a, 1)
    after_b = turn(own_b, -1)
    before_b = turn(own_b, 1)
    after_a = turn(own_a, -1)
    far = turn(before_a, 1), turn(after_b, -1)
    own, after, before = (own_a, own_b), (after_a, after_b), (before_a, before_b)

    mine = pack_set(merge_v, merge_t)
    other = move(mine[0], SWAP_CORE), move(mine[1], SWAP_CORE)
    first, second = pick(mine, other)
    first = move(first, Z_OUT)
    second = move(second, Z_OUT)
    third = move(first, Z_OUT)
    first_x = move(first, SWAP_CORE)
    second_x = move(second, SWAP_CORE)
    third_x = move(third, SWAP_CORE)

    near = leaf_near(own, after, before, trailing)
    weight, keep, send = leaf_top(near, far)
    got = move(send, SWAP_CORE)
    sets = prep(4, mine, other)
    *parts, up0 = merge_core(keep, got, sets)
    sets = lax.optimization_barrier((*sets, up0))[:4]
    parts = [parts[0]] + [move(parts[k], Z_TURN[k]) for k in (1, 2, 3)]
    sets = prep(0, mine, other, sets)
    sets = prep(3, (first, second), (first_x, second_x), sets)
    sets = prep(1, (second_x, first_x), (second, first), sets)
    sets = prep(2, (third, third_x), (third_x, third), sets)
    rest = leaf_rest(weight, own, after, before, far, trailing)

    low2, r0, *returns = merge_z(parts, sets)
    from_even = move(low2, X_UP)
    early = [move(returns[k - 1], Z_EARLY[k]) for k in (1, 2, 3)]
    got_up0 = move(up0, CORE_UP)
    low3, up3 = merge_x(merge_x3_body, from_even, low2, *sets)
    from_one = move(low3, X_ONE_TWO)
    from_three = move(low3, X_THREE_TWO)
    low4, own_top = merge_x(merge_x4_body, from_one, from_three, up3, *sets)
    home = [move(low4, X_HOME[k]) for k in range(4)]
    late = [move(own_top, Z_LATE[k]) for k in (1, 2, 3)]
    half = join(own_top, r0, *early, *late, *home)
    got_half = move(half, CORE_DOWN)
    return finish(half, got_half, up0, got_up0, rest)


def solution(mesh):
    return jax.shard_map(
        on_device,
        mesh=mesh,
        in_specs=(
            P("rows", "cols"),
            P("rows", "cols"),
            P("rows", "cols"),
            P("rows", None),
            P("rows", None),
        ),
        out_specs=P("rows", "cols"),
        check_vma=False,
    )
```

```python
import functools

import jax
import jax.numpy as jnp
from jax import lax
from jax.experimental import pallas as pl
from jax.experimental.pallas import tpu as pltpu
from jax.sharding import PartitionSpec as P


F32 = jnp.float32
BF16 = jnp.bfloat16
PANEL = 512
SET_ROWS = 1408
ANY = pl.BlockSpec(memory_space=pl.ANY)
VMEM = pl.BlockSpec(memory_space=pltpu.VMEM)


def route(pick):
    pairs = []
    for r in range(32):
        c, z, x = r & 1, (r >> 1) & 3, r >> 3
        to = pick(c, z, x)
        if to is not None:
            c, z, x = to
            pairs.append((r, (x % 4) * 8 + (z % 4) * 2 + c))
    return pairs


SWAP_CORE = route(lambda c, z, x: (1 - c, z, x))
CORE_UP = route(lambda c, z, x: (1, z, x) if c == 0 else None)
CORE_DOWN = route(lambda c, z, x: (0, z, x) if c == 1 else None)
Z_OUT = route(lambda c, z, x: (c, z - 1 if c else z + 1, x))
Z_TURN = {k: route(lambda c, z, x: (c, z + k, x)) for k in (1, 2, 3)}
Z_EARLY = {k: route(lambda c, z, x: (c, z + k, x) if (z + k) % 4 else None) for k in (1, 2, 3)}
Z_LATE = {k: route(lambda c, z, x: (c, 0, x) if x and (z + k) % 4 == 0 else None) for k in (1, 2, 3)}
X_UP = route(lambda c, z, x: (c, z, x + 1) if x % 2 == 0 else None)
X_ONE_TWO = route(lambda c, z, x: (c, z, 2) if x == 1 else None)
X_THREE_TWO = route(lambda c, z, x: (c, z, 2) if x == 3 else None)
X_HOME = {k: route(lambda c, z, x: (c, 0, 0) if x == 2 and (z + k) % 4 == 0 else None) for k in range(4)}


def move(block, pairs):
    return lax.ppermute(block, "rows", pairs)


def turn(block, by):
    count = lax.axis_size("cols")
    return lax.ppermute(block, "cols", [(i, (i + by) % count) for i in range(count)])


def split(block):
    high = block.astype(BF16)
    return high, (block - high.astype(F32)).astype(BF16)


def dot(left, right):
    return jnp.dot(left, right, preferred_element_type=F32)


def dot3(left, right):
    (lh, ll), (rh, rl) = left, right
    return dot(lh, rh) + (dot(lh, rl) + dot(ll, rh))


def dot_tall(left, right):
    (lh, ll), (rh, rl) = left, right
    n = lh.shape[0]
    both = dot(jnp.concatenate([lh, ll], 0), rh)
    return both[:n] + (both[n:] + dot(lh, rl))


def place():
    me = lax.axis_index("rows")
    return me % 2, (me // 2) % 4, me // 8


def shape(*dims, dtype=F32):
    return jax.ShapeDtypeStruct(dims, dtype)


def call(body, outs, flops, moved, mib, **options):
    return pl.pallas_call(
        body,
        out_shape=outs,
        cost_estimate=pl.CostEstimate(flops=flops, bytes_accessed=moved, transcendentals=0),
        compiler_params=pltpu.CompilerParams(vmem_limit_bytes=mib << 20),
        **options,
    )


def copy_all(sem, *pairs):
    copies = [pltpu.make_async_copy(src, dst, sem.at[i]) for i, (src, dst) in enumerate(pairs)]
    for copy in copies:
        copy.start()
    for copy in copies:
        copy.wait()


def pack_leaf_body(v, t, first, second, sem):
    copy_all(
        sem,
        (v.at[pl.ds(0, 768)], first),
        (v.at[pl.ds(768, 256)], second.at[pl.ds(0, 256)]),
        (t, second.at[pl.ds(256, 512)]),
    )


def pack_leaf(v, t):
    outs = (shape(768, 128), shape(768, 128))
    return call(
        pack_leaf_body,
        outs,
        0,
        3 << 19,
        1,
        in_specs=[ANY] * 2,
        out_specs=(VMEM,) * 2,
        scratch_shapes=[pltpu.SemaphoreType.DMA((3,))],
    )(v, t)


def pack_set_body(v, t, first, second, sem):
    copy_all(
        sem,
        (v.at[pl.ds(0, 704)], first),
        (v.at[pl.ds(704, 320)], second.at[pl.ds(0, 320)]),
        (t.at[pl.ds(0, 256)], second.at[pl.ds(320, 256)]),
        (t.at[pl.ds(256, 128), pl.ds(256, 256)], second.at[pl.ds(576, 128), pl.ds(0, 256)]),
        (t.at[pl.ds(384, 128), pl.ds(256, 256)], second.at[pl.ds(576, 128), pl.ds(256, 256)]),
    )


def pack_set(v, t):
    outs = (shape(704, PANEL), shape(704, PANEL))
    return call(
        pack_set_body,
        outs,
        0,
        6 << 20,
        1,
        in_specs=[ANY] * 2,
        out_specs=(VMEM,) * 2,
        scratch_shapes=[pltpu.SemaphoreType.DMA((5,))],
    )(v, t)


def masked(second, offset):
    rows = lax.broadcasted_iota(jnp.int32, (PANEL, 128), 0)
    cols = lax.broadcasted_iota(jnp.int32, (PANEL, 128), 1)
    return jnp.where(rows <= cols + offset * 128, second[256:], 0.0).T


def leaf_near_body(
    a0, b0, a1, b1, a3, b3, trailing, c_high, c_low, p_high, p_low, f_high, f_low, v_high, v_low, w_near, c_top
):
    c_top[...] = trailing[:PANEL]
    y = lax.axis_index("cols")
    slots = (0, 1, 3)
    shards = ((a0, b0), (a1, b1), (a3, b3))
    vt = [jnp.concatenate([a[...].T, b[:256].T], 1) for a, b in shards]
    vt = split(jnp.concatenate(vt, 0))
    for i, (k, (a, b)) in enumerate(zip(slots, shards)):
        part = slice(i * 128, (i + 1) * 128)
        f_high[part], f_low[part] = split(masked(b, (y + k) % 4))
        v_high[:, part], v_low[:, part] = split(a[:512])
    p_high[(y + 2) % 4] = jnp.zeros((128, 1024), BF16)
    p_low[(y + 2) % 4] = jnp.zeros((128, 1024), BF16)
    for j in range(4):
        part = slice(j * 256, (j + 1) * 256)
        c = split(trailing[:, part])
        c_high[:, part], c_low[:, part] = c
        p = split(dot3(vt, c))
        for i, k in enumerate(slots):
            at = slice(i * 128, (i + 1) * 128)
            p_high[(y + k) % 4, :, part] = p[0][at]
            p_low[(y + k) % 4, :, part] = p[1][at]
        p = [q[:, :, part].reshape(PANEL, 256) for q in (p_high, p_low)]
        w_near[:, part] = dot3((f_high[...], f_low[...]), p)


def leaf_near(own, after, before, trailing):
    outs = (
        *[shape(1024, 1024, dtype=BF16)] * 2,
        *[shape(4, 128, 1024, dtype=BF16)] * 2,
        *[shape(384, 512, dtype=BF16)] * 2,
        *[shape(512, 512, dtype=BF16)] * 2,
        shape(384, 1024),
        shape(512, 1024),
    )
    return call(leaf_near_body, outs, 3 * 1200000000, 7 << 20, 12)(*own, *after, *before, trailing)


def leaf_top_body(
    kept, c_high, c_low, _0, _1, f_high, f_low, _2, _3, w_near, c_top, a2, b2,
    w_out, top_out, p_high, p_low, v_high, v_low,
):
    far = (lax.axis_index("cols") + 2) % 4
    core = place()[0]
    base = (core if kept else 1 - core) * 512
    vt = split(jnp.concatenate([a2[...].T, b2[:256].T], 1))
    factor = split(masked(b2, far))
    lanes = pl.ds(pl.multiple_of(far * 128, 128), 128)
    near_far = f_high[:, lanes], f_low[:, lanes]
    v_high[:, 384:], v_low[:, 384:] = split(a2[:512])
    for j in range(2):
        part = pl.ds(pl.multiple_of(base + j * 256, 256), 256)
        to = slice(j * 256, (j + 1) * 256)
        p_far = split(dot_tall(vt, (c_high[:, part], c_low[:, part])))
        p_high[far, :, part], p_low[far, :, part] = p_far
        p = [q[:, :, part].reshape(PANEL, 256) for q in (p_high, p_low)]
        near = w_near[:, part] + dot3(near_far, p_far)
        weight = jnp.concatenate([near, dot_tall(factor, p)], 0)
        w_out[:, to] = weight
        top_out[:, to] = c_top[:, part] - dot3((v_high[...], v_low[...]), split(weight))


def leaf_top(kept, near, far):
    outs = (
        *[shape(512, 512)] * 2,
        *[shape(4, 128, 1024, dtype=BF16)] * 2,
        *[shape(512, 512, dtype=BF16)] * 2,
    )
    weight, top, p_high, p_low, v_high, v_low = call(
        functools.partial(leaf_top_body, kept),
        outs,
        3 * 500000000,
        8 << 20,
        6,
        input_output_aliases={2: 2, 3: 3, 6: 4, 7: 5},
    )(*near, *far)
    near = (*near[:2], p_high, p_low, *near[4:6], v_high, v_low, *near[8:])
    return weight, top, near


def leaf_rest_body(w_keep, w_send, a0, b0, a1, b1, a3, b3, a2, b2, trailing, out):
    core = place()[0]
    shards = ((a0, b0), (a1, b1), (a3, b3), (a2, b2))
    vectors = [jnp.concatenate([a[512:], b[:256]], 0) for a, b in shards]
    vectors = split(jnp.concatenate(vectors, 1))

    def step(j, carry):
        at = pl.ds(pl.multiple_of(j * 256, 256), 256)
        for half, weight in ((core, w_keep), (1 - core, w_send)):
            part = pl.ds(pl.multiple_of(half * 512 + j * 256, 256), 256)
            out[:, part] = trailing[:, part] - dot3(vectors, split(weight[:, at]))
        return carry

    lax.fori_loop(0, 2, step, 0)


def leaf_rest(w_keep, w_send, own, after, before, far, trailing):
    bottom = pl.BlockSpec((512, 1024), lambda i: (1, 0))

    def whole(a):
        return pl.BlockSpec(a.shape, lambda i: (0, 0))

    args = (w_keep, w_send, *own, *after, *before, *far)
    return call(
        leaf_rest_body,
        shape(1024, 1024),
        3 * 536870912,
        10 << 20,
        20,
        grid=(1,),
        in_specs=[whole(a) for a in args] + [bottom],
        out_specs=bottom,
    )(*args, trailing)


def set_shapes(count):
    return (
        *[shape(count, 1024, 512, dtype=BF16)] * 2,
        *[shape(count, 512, 1024, dtype=BF16)] * 2,
    )


def pick_body(a0, b0, a1, b1, first, second, sem):
    core = place()[0]

    def copies(one, two):
        return [
            pltpu.make_async_copy(one, first, sem.at[0]),
            pltpu.make_async_copy(two, second, sem.at[1]),
        ]

    @pl.when(core == 0)
    def _():
        for copy in copies(a0, b0):
            copy.start()

    @pl.when(core != 0)
    def _():
        for copy in copies(b1, a1):
            copy.start()

    for copy in copies(a0, b0):
        copy.wait()


def pick(mine, other):
    return call(
        pick_body,
        (shape(704, PANEL),) * 2,
        0,
        6 << 20,
        1,
        in_specs=[ANY] * 4,
        out_specs=(ANY,) * 2,
        scratch_shapes=[pltpu.SemaphoreType.DMA((2,))],
    )(*mine, *other)


def prep_body(slot, *refs):
    (a0, b0, a1, b1), refs = refs[:4], refs[4:]
    ab_high, ab_low, wt_high, wt_low, block, sem = refs[-6:]
    core, z, _ = place()
    half = SET_ROWS // 2

    def copies(one, two):
        return [
            pltpu.make_async_copy(one, block.at[pl.ds(0, half)], sem.at[0]),
            pltpu.make_async_copy(two, block.at[pl.ds(half, half)], sem.at[1]),
        ]

    on_core = 1 if slot == 4 else 0

    @pl.when(core == on_core)
    def _():
        for copy in copies(a0, b0):
            copy.start()

    @pl.when(core != on_core)
    def _():
        for copy in copies(a1, b1):
            copy.start()

    for copy in copies(a0, b0):
        copy.wait()
    index = 0 if slot == 4 else (z + slot) % 4
    rows = lax.broadcasted_iota(jnp.int32, (256, 512), 0)
    cols = lax.broadcasted_iota(jnp.int32, (256, 512), 1)
    upper = split(jnp.where(rows <= cols, block[1024:1280], 0.0))
    corner = jnp.concatenate([block[1280:, :256], block[1280:, 256:]], 0)
    corner = split(jnp.where(rows[:, :256] <= cols[:, :256], corner, 0.0))

    def step(i, carry):
        part = pl.ds(pl.multiple_of(i * 256, 256), 256)
        high, low = split(block[part])
        ab_high[index, part], ab_low[index, part] = high, low
        product = dot3((high[:, :256], low[:, :256]), upper)
        right = product[:, 256:] + dot3((high[:, 256:], low[:, 256:]), corner)
        wt_high[index, :256, part], wt_low[index, :256, part] = split(product[:, :256].T)
        wt_high[index, 256:, part], wt_low[index, 256:, part] = split(right.T)
        return carry

    lax.fori_loop(0, 4, step, 0, unroll=True)


def prep(slot, on_core, off_core, sets=()):
    return call(
        functools.partial(prep_body, slot),
        set_shapes(1 if slot == 4 else 4),
        3 * 2 * 1024 * 512 * 384,
        7 << 20,
        8,
        in_specs=[ANY] * 4 + [VMEM] * len(sets),
        out_specs=(VMEM,) * 4,
        input_output_aliases={4 + i: i for i in range(len(sets))},
        scratch_shapes=[pltpu.VMEM((SET_ROWS, PANEL), F32), pltpu.SemaphoreType.DMA((2,))],
    )(*on_core, *off_core, *sets)


def dot_wide(left, right):
    (lh, ll), (rh, rl) = left, right
    n = rh.shape[1]
    if n > 128:
        return dot3(left, right)
    both = dot(lh, jnp.concatenate([rh, rl], 1))
    return both[:, :n] + (both[:, n:] + dot(ll, rh))


def apply(sets, index, low, up):
    ab_high, ab_low, wt_high, wt_low = sets
    (low_h, low_l), (up_h, up_l) = split(low), split(up)
    tops = jnp.concatenate([low_h, up_h], 0), jnp.concatenate([low_l, up_l], 0)
    weight = split(dot_wide((wt_high[index], wt_low[index]), tops))
    low = low - dot_wide((ab_high[index, :512], ab_low[index, :512]), weight)
    up = up - dot_wide((ab_high[index, 512:], ab_low[index, 512:]), weight)
    return low, up


def merge_core_body(keep, got, s0, s1, s2, s3, o0, o1, o2, o3, up_out, low_v):
    core, z, _ = place()
    first = core == 0
    low = jnp.where(first, keep[...], got[...])
    up = jnp.where(first, got[...], keep[...])
    low, up_out[...] = apply((s0, s1, s2, s3), 0, low, up)
    for q in range(4):
        low_v[q] = low[:, q * 128 : (q + 1) * 128]
    for k, out in enumerate((o0, o1, o2, o3)):
        out[...] = low_v[(z + k) % 4]


PIECE = shape(512, 128)


def merge_core(keep, got, sets):
    return call(
        merge_core_body,
        (*[PIECE] * 4, shape(512, 512)),
        3 * 2 * 1024 * 512 * 1024,
        8 << 20,
        8,
        scratch_shapes=[pltpu.VMEM((4, 512, 128), F32)],
    )(keep, got, *sets)


def merge_z_body(g0, g1, g2, g3, s0, s1, s2, s3, low_out, r0, r1, r2, r3, tops):
    _, z, _ = place()
    for k, got in enumerate((g0, g1, g2, g3)):
        tops[(z + 4 - k) % 4] = got[...]
    for index, a, b in ((1, 0, 1), (3, 2, 3), (2, 0, 2)):
        tops[a], tops[b] = apply((s0, s1, s2, s3), index, tops[a], tops[b])
    low_out[...] = tops[0]
    for k, out in enumerate((r0, r1, r2, r3)):
        out[...] = tops[(z + k) % 4]


def merge_z(parts, sets):
    return call(
        merge_z_body,
        (PIECE,) * 5,
        3 * 3 * 2 * 1024 * 512 * 256,
        14 << 20,
        4,
        scratch_shapes=[pltpu.VMEM((4, 512, 128), F32)],
    )(*parts, *sets)


def merge_x3_body(low, up, s0, s1, s2, s3, low_out, up_out):
    low_out[...], up_out[...] = apply((s0, s1, s2, s3), 0, low[...], up[...])


def merge_x4_body(low, up, up3, s0, s1, s2, s3, low_out, own_out):
    low_out[...], up4 = apply((s0, s1, s2, s3), 0, low[...], up[...])
    own_out[...] = jnp.where(place()[2] == 2, up4, up3[...])


def merge_x(body, *args):
    return call(body, (PIECE, PIECE), 3 * 2 * 1024 * 512 * 256, 5 << 20, 3)(*args)


def join_body(own, r0, e1, e2, e3, l1, l2, l3, h0, h1, h2, h3, out):
    _, z, x = place()

    def put(parts):
        for k, source in enumerate(parts):
            out[:, pl.ds(pl.multiple_of(((z + 4 - k) % 4) * 128, 128), 128)] = source[...]

    @pl.when(z != 0)
    def _():
        put((r0, e1, e2, e3))

    @pl.when((z == 0) & (x != 0))
    def _():
        put((own, l1, l2, l3))

    @pl.when((z == 0) & (x == 0))
    def _():
        put((h0, h1, h2, h3))


def join(*parts):
    return call(join_body, shape(512, 512), 0, 4 << 20, 1)(*parts)


def finish_body(half, got_half, up, got_up, rest, out, sem):
    core = place()[0]

    def copies(left, right):
        return [
            pltpu.make_async_copy(left, out.at[pl.ds(0, 512), pl.ds(0, 512)], sem.at[0]),
            pltpu.make_async_copy(right, out.at[pl.ds(0, 512), pl.ds(512, 512)], sem.at[1]),
        ]

    @pl.when(core == 0)
    def _():
        for copy in copies(half, got_half):
            copy.start()

    @pl.when(core != 0)
    def _():
        for copy in copies(got_up, up):
            copy.start()

    for copy in copies(half, got_half):
        copy.wait()


def finish(half, got_half, up, got_up, rest):
    return call(
        finish_body,
        shape(1024, 1024),
        0,
        6 << 20,
        6,
        in_specs=[VMEM] * 4 + [ANY],
        out_specs=ANY,
        input_output_aliases={4: 0},
        scratch_shapes=[pltpu.SemaphoreType.DMA((2,))],
    )(half, got_half, up, got_up, rest)


def on_device(trailing, leaf_v, leaf_t, merge_v, merge_t):
    own_a, own_b = pack_leaf(leaf_v, leaf_t)
    before_a = turn(own_a, 1)
    after_b = turn(own_b, -1)
    before_b = turn(own_b, 1)
    after_a = turn(own_a, -1)
    far = turn(before_a, 1), turn(after_b, -1)
    own, after, before = (own_a, own_b), (after_a, after_b), (before_a, before_b)

    mine = pack_set(merge_v, merge_t)
    other = move(mine[0], SWAP_CORE), move(mine[1], SWAP_CORE)
    first, second = pick(mine, other)
    first = move(first, Z_OUT)
    second = move(second, Z_OUT)
    third = move(first, Z_OUT)
    first_x = move(first, SWAP_CORE)
    second_x = move(second, SWAP_CORE)
    third_x = move(third, SWAP_CORE)

    core_sets = prep(4, mine, other)
    near = leaf_near(own, after, before, trailing)
    w_send, send, near = leaf_top(False, near, far)
    got = move(send, SWAP_CORE)
    w_keep, keep, _ = leaf_top(True, near, far)
    *parts, up0 = merge_core(keep, got, core_sets)
    parts = [parts[0]] + [move(parts[k], Z_TURN[k]) for k in (1, 2, 3)]
    sets = prep(0, mine, other)
    sets = prep(3, (first, second), (first_x, second_x), sets)
    sets = prep(1, (second_x, first_x), (second, first), sets)
    sets = prep(2, (third, third_x), (third_x, third), sets)
    rest = leaf_rest(w_keep, w_send, own, after, before, far, trailing)

    low2, r0, *returns = merge_z(parts, sets)
    from_even = move(low2, X_UP)
    early = [move(returns[k - 1], Z_EARLY[k]) for k in (1, 2, 3)]
    got_up0 = move(up0, CORE_UP)
    low3, up3 = merge_x(merge_x3_body, from_even, low2, *sets)
    from_one = move(low3, X_ONE_TWO)
    from_three = move(low3, X_THREE_TWO)
    low4, own_top = merge_x(merge_x4_body, from_one, from_three, up3, *sets)
    home = [move(low4, X_HOME[k]) for k in range(4)]
    late = [move(own_top, Z_LATE[k]) for k in (1, 2, 3)]
    half = join(own_top, r0, *early, *late, *home)
    got_half = move(half, CORE_DOWN)
    return finish(half, got_half, up0, got_up0, rest)


def solution(mesh):
    return jax.shard_map(
        on_device,
        mesh=mesh,
        in_specs=(
            P("rows", "cols"),
            P("rows", "cols"),
            P("rows", "cols"),
            P("rows", None),
            P("rows", None),
        ),
        out_specs=P("rows", "cols"),
        check_vma=False,
    )
```
